32 devices in a mesh: dp: 4 (over z), expert: 4 (over y, x), seq: 2 (over core).
Axes of the slice: x: 2, y: 2, z: 4, core: 2. Of those that a mesh axis runs over, the one named last changes fastest.
Arguments:
- tokens: bfloat16 [4096, 2048], P(('dp', 'expert', 'seq')), may hold values from -6 to 6
- out_grad: bfloat16 [4096, 2048], P(('dp', 'expert', 'seq')), may hold values from -6 to 6
- expert_ids: int32 [4096, 2], P(('dp', 'expert', 'seq')), may hold values from 0 to 3, all different within a row; in each aligned block of 128 rows (0 to 127, 128 to 255, ...) at most 96 rows name the same one
- gate_values: float32 [4096, 2], P(('dp', 'expert', 'seq')), may hold values from 0.2 to 1
- gate_weight: bfloat16 [4, 2048, 512], P('expert', 'dp', 'seq'), may hold values from -0.125 to 0.125
- up_weight: bfloat16 [4, 2048, 512], P('expert', 'dp', 'seq'), may hold values from -0.125 to 0.125
- down_weight: bfloat16 [4, 2048, 512], P('expert', 'dp', 'seq'), may hold values from -0.25 to 0.25
Outputs:
- in_grad: bfloat16 [4096, 2048], P(('dp', 'expert', 'seq'))
- gate_grads: float32 [4096, 2], P(('dp', 'expert', 'seq'))
- gate_weight_grad: bfloat16 [4, 2048, 512], P('expert', 'dp', 'seq')
- up_weight_grad: bfloat16 [4, 2048, 512], P('expert', 'dp', 'seq')
- down_weight_grad: bfloat16 [4, 2048, 512], P('expert', 'dp', 'seq')
The draws below stay inside these ranges and needn't reach their ends.
Inputs may be any that keep to these rules, and one draw needn't show every extreme that they name: `expert_ids`: the two ids of a row differ. Within the 128 rows of one device no expert is named more than 96 times, a bound that some block reaches.
All inputs are finite; a program needn't handle non-finite values.
Results may differ from the reference program's by a relative error of at most 0.017.
Values may be sent and summed in bfloat16 or wider, within the bound.
No kernel may reach another device: no remote copies, remote signals or barrier semaphores. Data moves between devices by JAX's collectives and lax.ppermute only.
A program may use at most 64 MiB of HBM per device.

```python
import math
import jax
import jax.numpy as jnp
import numpy as np
from jax import lax

D = 2048
HW = 512
TOK_DEV = 128
EXPERTS = 4
CAP = 96
TOKENS = 4096
N_DP = 4
N_SEQ = 2


def spiked(entries, own_key, source, target, blocks, factor):
    def block_of(dim):
        return (jnp.arange(entries.shape[dim]) // (entries.shape[dim] // blocks)).reshape((-1,) + (1,) * (entries.ndim - 1 - dim))

    one_side = jax.random.permutation(own_key, blocks)[block_of(target)]
    other_side = (block_of(target) + blocks // 2) % blocks
    return jnp.where((block_of(source) == one_side) | (block_of(source) == other_side), factor * entries, entries)


def levels(own_key, dims, shards, smallest, high):
    gain, own = 1.0, jax.random.fold_in(own_key, 6)
    for dim, shards_of in shards:
        draws = jnp.exp(jax.random.uniform(jax.random.fold_in(own, dim), (shards_of,), jnp.float32, smallest / len(shards), high / len(shards)))
        gain = gain * jnp.repeat(draws, dims[dim] // shards_of).reshape([-1 if axis == dim else 1 for axis in range(len(dims))])
    return gain


def assign_block(own_key, own, number, rows, number_of, top, reach, slope):
    sequence = jax.random.permutation(own_key, number_of)
    heavy_load, ordinary = shares(number_of, rows * top, reach, slope, True), shares(number_of, rows * top, reach, slope, False)
    places = jnp.arange(number_of)

    def named(sizes, turn):
        used = int((sizes > 0).sum())
        fixed = max(1, used // 4)
        shifted = fixed + (places - fixed + turn * (used - fixed)) % max(1, number_of - fixed)
        return jnp.zeros((number_of,), jnp.int32).at[sequence[jnp.where(places < fixed, places, shifted)]].set(jnp.asarray(sizes, jnp.int32))

    sizes = jnp.where(number % 4 == 0, named(heavy_load, number // 4), named(ordinary, number - number // 4 - 1))
    mixed = jax.random.permutation(jax.random.fold_in(own, 3), number_of)
    donor, taker = mixed[0:number_of // 2 * 2:2], mixed[1:number_of // 2 * 2:2]
    room = jnp.minimum(sizes[donor] - 1, reach - sizes[taker]) // 2
    room = jnp.where((donor == sequence[0]) | (taker == sequence[0]) | (sizes[taker] == 0), 0, jnp.maximum(room, 0))
    shifted = jax.random.randint(jax.random.fold_in(own, 4), (number_of // 2,), 0, 1 << 20) % (room + 1)
    sizes = sizes.at[donor].add(-shifted).at[taker].add(shifted)
    members = jnp.searchsorted(jnp.cumsum(sizes), jnp.arange(rows * top), side="right").astype(jnp.int32)
    table = members.reshape(top, rows).T
    table = table[jax.random.permutation(jax.random.fold_in(own, 1), rows)]
    turn = jax.random.randint(jax.random.fold_in(own, 2), (rows, 1), 0, top)
    return jnp.take_along_axis(table, (jnp.arange(top)[None, :] + turn) % top, axis=1)


def shares(amount, total, limit, lean, full):
    loads = [(1 << 20) // math.isqrt(rank ** lean) + 1 for rank in range(1, amount + 1)]
    largest = limit if full else min(limit, max(-(-total // amount), total * loads[0] // sum(loads)))
    least = 1 if total - largest >= amount - 1 else 0
    counts, rest = [largest] + [least] * (amount - 1), total - largest - least * (amount - 1)
    while rest > 0:
        candidates = [i for i in range(1, amount) if counts[i] < largest] or [i for i in range(1, amount) if counts[i] < limit]
        mass, left = sum([loads[i] for i in candidates]), rest
        for i in candidates:
            extra = min(limit - counts[i], max(1, left * loads[i] // mass), rest)
            counts[i] = counts[i] + extra
            rest = rest - extra
    return np.array(counts)


def noise(key, dims, deviation, limit, shards=(), held_as=jnp.bfloat16):
    values = jax.random.normal(key, dims, jnp.float32) * deviation
    if len(shards) > 0:
        values = levels(key, dims, shards, -0.22, 0.18) * values
    return jnp.clip(values, min=-limit, max=limit).astype(held_as)


def heavy_noise(stream_key, shape, width, limit, cuts, heavy, kind=jnp.bfloat16):
    result = width * jax.random.normal(stream_key, shape, jnp.float32)
    if cuts:
        result = result * levels(stream_key, shape, cuts, -0.22, 0.18)
    return jnp.clip(spiked(result, jax.random.fold_in(stream_key, 3), *heavy), -limit, limit).astype(kind)


def setup_inputs(seed: int = 0) -> dict:
    keys = jax.random.split(jax.random.key(seed), 8)
    tokens = noise(keys[0], (TOKENS, D), 1.0, 6.0, ((0, 32),))
    out_grad = heavy_noise(keys[1], (TOKENS, D), 1.0, 6.0, ((0, 32),), (0, 1, 32, 2.75))
    expert_ids_keys = jax.random.split(jax.random.fold_in(keys[2], 1), TOKENS // TOK_DEV)
    expert_ids_turns = jax.random.permutation(jax.random.fold_in(keys[2], 3), TOKENS // TOK_DEV)
    expert_ids = jax.vmap(lambda own, number: assign_block(jax.random.fold_in(keys[2], 2), own, number, TOK_DEV, EXPERTS, 2, CAP, 2))(expert_ids_keys, expert_ids_turns).reshape((TOKENS, 2))
    gate_values = jnp.clip(0.2 + 0.8 * jax.random.uniform(keys[3], (TOKENS, 2), jnp.float32) ** levels(keys[3], (TOKENS, 2), ((0, 32),), -0.2, 0.2), 0.2, 1.0)
    gate_weight = noise(keys[4], (EXPERTS, D, HW), D ** -0.5, 0.125, ((0, 4), (1, 4), (2, 2)))
    up_weight = noise(keys[5], (EXPERTS, D, HW), D ** -0.5, 0.125, ((0, 4), (1, 4), (2, 2)))
    down_weight = noise(keys[6], (EXPERTS, D, HW), HW ** -0.5, 0.25, ((0, 4), (1, 4), (2, 2)))
    return dict(tokens=tokens, out_grad=out_grad, expert_ids=expert_ids, gate_values=gate_values, gate_weight=gate_weight, up_weight=up_weight, down_weight=down_weight)


def route_slots(block_ids, expert_count, capacity):
    flat_ids = block_ids.reshape(-1).astype(jnp.int32)
    onehot = (flat_ids[:, None] == jnp.arange(expert_count, dtype=jnp.int32)[None, :]).astype(jnp.int32)
    position = jnp.sum((jnp.cumsum(onehot, axis=0) - 1) * onehot, axis=1)
    return (flat_ids * capacity + position).astype(jnp.int32)


def expert_half(routed, grads_in, gate_vals, gate_cols, up_cols, down_cols):
    contract_last = (((1,), (1,)), ((), ()))
    gate_pre = jnp.dot(routed, gate_cols, preferred_element_type=jnp.float32)
    up_pre = jnp.dot(routed, up_cols, preferred_element_type=jnp.float32)
    sigmoid_val = jax.nn.sigmoid(gate_pre)
    activated = gate_pre * sigmoid_val
    hidden = (activated * up_pre).astype(jnp.bfloat16)
    produced = lax.dot_general(hidden, down_cols, contract_last, preferred_element_type=jnp.float32)
    gate_inner = jnp.sum(grads_in.astype(jnp.float32) * produced, axis=1)
    scaled = (gate_vals[:, None] * grads_in.astype(jnp.float32)).astype(jnp.bfloat16)
    hidden_grad = jnp.dot(scaled, down_cols, preferred_element_type=jnp.float32)
    gate_grad = (hidden_grad * up_pre * sigmoid_val * (1.0 + gate_pre * (1.0 - sigmoid_val))).astype(jnp.bfloat16)
    up_grad = (hidden_grad * activated).astype(jnp.bfloat16)
    back_sum = lax.dot_general(gate_grad, gate_cols, contract_last, preferred_element_type=jnp.float32)
    back_sum = back_sum + lax.dot_general(up_grad, up_cols, contract_last, preferred_element_type=jnp.float32)
    return hidden, scaled, gate_grad, up_grad, back_sum.astype(jnp.bfloat16), gate_inner


def group_sum(left_rows, right_rows):
    left_groups = left_rows.reshape(N_DP, -1, left_rows.shape[1]).astype(jnp.float32)
    right_groups = right_rows.reshape(N_DP, -1, right_rows.shape[1]).astype(jnp.float32)
    partial_sums = jnp.einsum("grd,grh->gdh", left_groups, right_groups, precision=lax.Precision.HIGHEST)
    rounded = lax.optimization_barrier(partial_sums.astype(jnp.bfloat16))
    return jnp.sum(rounded.astype(jnp.float32), axis=0).astype(jnp.bfloat16)


def reference(tokens, out_grad, expert_ids, gate_values, gate_weight, up_weight, down_weight):
    block_count = TOKENS // TOK_DEV
    half_width = HW // N_SEQ
    blocks = expert_ids.reshape(block_count, TOK_DEV * 2)
    slot_index = jax.vmap(lambda block_ids: route_slots(block_ids, EXPERTS, CAP))(blocks)
    block_number = jnp.arange(block_count, dtype=jnp.int32)[:, None]
    global_place = (slot_index // CAP) * (block_count * CAP) + block_number * CAP + slot_index % CAP
    pair_table = jnp.full((EXPERTS * block_count * CAP,), 2 * TOKENS, jnp.int32)
    pair_table = pair_table.at[global_place.reshape(-1)].set(jnp.arange(2 * TOKENS, dtype=jnp.int32))
    pair_table = pair_table.reshape(EXPERTS, block_count * CAP)
    flat_gates = gate_values.reshape(-1)

    def per_expert(totals, packed):
        input_total, gate_total = totals
        pair_list, gate_full, up_full, down_full = packed
        token_list = pair_list // 2
        routed = jnp.take(tokens, token_list, axis=0, mode="fill", fill_value=0)
        grads_in = jnp.take(out_grad, token_list, axis=0, mode="fill", fill_value=0)
        gate_vals = jnp.take(flat_gates, pair_list, axis=0, mode="fill", fill_value=0)
        slot_sum = jnp.zeros(routed.shape, jnp.float32)
        inner_sum = jnp.zeros((routed.shape[0],), jnp.float32)
        gate_parts, up_parts, down_parts = [], [], []
        for half_index in range(N_SEQ):
            lower = half_index * half_width
            upper = lower + half_width
            hidden, scaled, gate_grad, up_grad, back_grad, gate_inner = expert_half(
                routed, grads_in, gate_vals, gate_full[:, lower:upper], up_full[:, lower:upper], down_full[:, lower:upper])
            slot_sum = slot_sum + back_grad.astype(jnp.float32)
            inner_sum = inner_sum + gate_inner
            gate_parts.append(group_sum(routed, gate_grad))
            up_parts.append(group_sum(routed, up_grad))
            down_parts.append(group_sum(scaled, hidden))
        slot_grad = slot_sum.astype(jnp.bfloat16)
        input_total = input_total.at[token_list].add(slot_grad.astype(jnp.float32), mode="drop")
        gate_total = gate_total.at[pair_list].set(inner_sum, mode="drop")
        outputs = (jnp.concatenate(gate_parts, axis=1), jnp.concatenate(up_parts, axis=1), jnp.concatenate(down_parts, axis=1))
        return (input_total, gate_total), outputs

    start_totals = (jnp.zeros((TOKENS, D), jnp.float32), jnp.zeros((2 * TOKENS,), jnp.float32))
    final_totals, weight_grads = lax.scan(per_expert, start_totals, (pair_table, gate_weight, up_weight, down_weight))
    in_grad = final_totals[0].astype(jnp.bfloat16)
    gate_grads = final_totals[1].reshape(TOKENS, 2)
    return in_grad, gate_grads, weight_grads[0], weight_grads[1], weight_grads[2]
```

```python
from functools import partial

import jax
import jax.numpy as jnp
from jax import lax
from jax.sharding import PartitionSpec as P

from jax.experimental import pallas as pl
from jax.experimental.pallas import tpu as pltpu

ROLES = 5
EXT = 128
CONTRACT_FIRST = (((0,), (0,)), ((), ()))
CONTRACT_LAST = (((1,), (1,)), ((), ()))


def start_blocks(sources, target, sems, first=0):
    copies = []
    row = 0
    for number, source in enumerate(sources):
        rows = source.shape[0]
        copy = pltpu.make_async_copy(
            source, target.at[pl.ds(row, rows), :], sems.at[first + number]
        )
        copy.start()
        copies.append(copy)
        row += rows
    return copies


def start_weights(place, sources, target, sems, first):
    own, across, from_right, from_left, far = sources
    rows = own.shape[0]

    def slot(shift):
        at = pl.multiple_of(lax.rem(place + shift, 4) * rows, rows)
        return target.at[pl.ds(at, rows), :]

    own_copy = pltpu.make_async_copy(own, slot(0), sems.at[first])
    across_copy = pltpu.make_async_copy(across, slot(2), sems.at[first + 1])
    own_copy.start()
    across_copy.start()

    @pl.when(place == 3)
    def _():
        pltpu.make_async_copy(far, slot(1), sems.at[first + 2]).start()

    @pl.when(place != 3)
    def _():
        pltpu.make_async_copy(from_right, slot(1), sems.at[first + 2]).start()

    @pl.when(place == 0)
    def _():
        pltpu.make_async_copy(far, slot(3), sems.at[first + 3]).start()

    @pl.when(place != 0)
    def _():
        pltpu.make_async_copy(from_left, slot(3), sems.at[first + 3]).start()

    return [
        own_copy,
        across_copy,
        pltpu.make_async_copy(from_right, slot(1), sems.at[first + 2]),
        pltpu.make_async_copy(from_left, slot(3), sems.at[first + 3]),
    ]


def send_roles(place, held, outs, sems):
    owners = (
        place,
        3 - place,
        lax.rem(place + 2, 4),
        jnp.minimum(place + 1, 3),
        jnp.maximum(place - 1, 0),
    )
    copies = [
        pltpu.make_async_copy(held.at[owner], out, sems.at[number])
        for number, (owner, out) in enumerate(zip(owners, outs))
    ]
    for copy in copies:
        copy.start()
    for copy in copies:
        copy.wait()


def gate_column(ext, expert, expert_count):
    lane = lax.broadcasted_iota(jnp.int32, ext.shape, 1)
    mine = (lane == expert) | (lane == expert_count + expert)
    return jnp.sum(jnp.where(mine, ext.astype(jnp.float32), 0.0), axis=1, keepdims=True)


def hidden_kernel(place_ref, *refs, blocks, expert_count):
    x_refs, g_refs = refs[:blocks], refs[blocks : 2 * blocks]
    w_refs = refs[2 * blocks : 2 * blocks + 5]
    gate_fac, up_fac, hid = refs[2 * blocks + 5 : 2 * blocks + 8]
    outs = refs[2 * blocks + 8 : 2 * blocks + 8 + ROLES]
    x_all, g_all, w_all, scaled_hid, held, sems = refs[2 * blocks + 8 + ROLES :]
    place, expert = place_ref[0], place_ref[1]
    w_copies = start_weights(place, w_refs, w_all, sems, 0)
    x_copies = start_blocks(x_refs, x_all, sems, 4)
    g_copies = start_blocks(g_refs, g_all, sems, 4 + blocks)
    width = x_all.shape[1]
    half = gate_fac.shape[1]
    for copy in w_copies:
        copy.wait()
    per = blocks // 2
    rows = x_all.shape[0] // 2
    for part in range(2):
        for copy in x_copies[part * per : (part + 1) * per]:
            copy.wait()
        span = slice(part * rows, (part + 1) * rows)
        pre = jnp.dot(x_all[span, :], w_all[...], preferred_element_type=jnp.float32)
        pre_gate, pre_up = pre[:, :half], pre[:, half:]
        sig = jax.nn.sigmoid(pre_gate)
        active = pre_gate * sig
        hidden = active * pre_up
        gate_fac[span, :] = pre_up * sig * (1.0 + pre_gate * (1.0 - sig))
        up_fac[span, :] = active
        hid[span, :] = hidden
    for copy in g_copies:
        copy.wait()
    gates = gate_column(g_all[:, width:], expert, expert_count)
    scaled_hid[...] = (gates * hid[...]).astype(jnp.bfloat16)
    count, _, cols = held.shape
    for owner in range(count):
        held[owner] = lax.dot_general(
            scaled_hid[...],
            g_all[:, owner * cols : (owner + 1) * cols],
            CONTRACT_FIRST,
            preferred_element_type=jnp.float32,
        ).astype(jnp.bfloat16)
    send_roles(place, held, outs, sems)


def grads_kernel(place_ref, *refs, blocks, expert_count):
    x_refs, g_refs = refs[:blocks], refs[blocks : 2 * blocks]
    c_refs = refs[2 * blocks : 2 * blocks + 5]
    gate_fac, up_fac, hid = refs[2 * blocks + 5 : 2 * blocks + 8]
    pair, inner = refs[2 * blocks + 8 : 2 * blocks + 10]
    outs = refs[2 * blocks + 10 : 2 * blocks + 10 + ROLES]
    x_all, g_all, c_all, held, sems = refs[2 * blocks + 10 + ROLES :]
    place, expert = place_ref[0], place_ref[1]
    c_copies = start_weights(place, c_refs, c_all, sems, 0)
    g_copies = start_blocks(g_refs, g_all, sems, 4 + blocks)
    x_copies = start_blocks(x_refs, x_all, sems, 4)
    width = x_all.shape[1]
    half = gate_fac.shape[1]
    for copy in c_copies:
        copy.wait()
    per = blocks // 2
    rows = x_all.shape[0] // 2
    for part in range(2):
        for copy in g_copies[part * per : (part + 1) * per]:
            copy.wait()
        span = slice(part * rows, (part + 1) * rows)
        seen = jnp.dot(g_all[span, :width], c_all[...], preferred_element_type=jnp.float32)
        gates = gate_column(g_all[span, width:], expert, expert_count)
        hidden_grad = gates * seen
        pair[span, :half] = (hidden_grad * gate_fac[span, :]).astype(jnp.bfloat16)
        pair[span, half:] = (hidden_grad * up_fac[span, :]).astype(jnp.bfloat16)
        total = jnp.sum(hid[span, :] * seen, axis=1, keepdims=True)
        high = total.astype(jnp.bfloat16).astype(jnp.float32)
        lane = lax.broadcasted_iota(jnp.int32, (rows, EXT), 1)
        inner[span, :] = jnp.where(
            lane == 0, high, jnp.where(lane == 1, total - high, 0.0)
        ).astype(jnp.bfloat16)
    for copy in x_copies:
        copy.wait()
    count, _, cols = held.shape
    for owner in range(count):
        held[owner] = lax.dot_general(
            pair[...],
            x_all[:, owner * cols : (owner + 1) * cols],
            CONTRACT_FIRST,
            preferred_element_type=jnp.float32,
        ).astype(jnp.bfloat16)
    send_roles(place, held, outs, sems)


def back_kernel(place_ref, *refs):
    w_refs = refs[:5]
    pair, inner, same, other, w_all, sems = refs[5:]
    copies = start_weights(place_ref[0], w_refs, w_all, sems, 0)
    for copy in copies:
        copy.wait()
    rows = same.shape[0]
    width = w_all.shape[0]
    for part, out in ((1, other), (0, same)):
        span = slice(part * rows, (part + 1) * rows)
        out[:, :width] = lax.dot_general(
            pair[span, :], w_all[...], CONTRACT_LAST, preferred_element_type=jnp.float32
        ).astype(jnp.bfloat16)
        out[:, width:] = inner[span, :]


ANY = pl.BlockSpec(memory_space=pl.ANY)
ON_CHIP = pl.BlockSpec(memory_space=pltpu.VMEM)
ON_SCALAR = pl.BlockSpec(memory_space=pltpu.SMEM)


def shape_of(dims, kind=jnp.bfloat16):
    return jax.ShapeDtypeStruct(dims, kind)


RIGHT = [(0, 1), (1, 2), (2, 3)]
LEFT = [(1, 0), (2, 1), (3, 2)]
ACROSS = [(0, 2), (2, 0), (1, 3), (3, 1)]
FAR_IN = [(2, 3), (1, 0)]
FAR_OUT = [(0, 1), (3, 2)]
FLIP_X = [(0, 1), (1, 0), (2, 3), (3, 2)]
FLIP_Y = [(0, 2), (2, 0), (1, 3), (3, 1)]
FLIP_XY = [(0, 3), (3, 0), (1, 2), (2, 1)]
SWAP = [(0, 1), (1, 0)]


def moved(name, value, axis, pairs):
    with jax.named_scope(name):
        return lax.ppermute(value, axis, pairs)


def gathered(tag, shard):
    across = moved(tag + "_across", shard, "dp", ACROSS)
    from_left = moved(tag + "_right", shard, "dp", RIGHT)
    from_right = moved(tag + "_left", shard, "dp", LEFT)
    far = moved(tag + "_far", across, "dp", FAR_IN)
    return [shard, across, from_right, from_left, far]


def scattered(tag, roles):
    own, far, across, to_right, to_left = roles
    far_in = moved(tag + "_far", far, "dp", FAR_OUT)
    from_left = moved(tag + "_right", to_right, "dp", RIGHT)
    from_right = moved(tag + "_left", to_left, "dp", LEFT)
    relayed = (across.astype(jnp.float32) + far_in.astype(jnp.float32)).astype(jnp.bfloat16)
    across_in = moved(tag + "_across", relayed, "dp", ACROSS)
    total = own.astype(jnp.float32) + from_left.astype(jnp.float32)
    total = total + from_right.astype(jnp.float32) + across_in.astype(jnp.float32)
    return total.astype(jnp.bfloat16).T


def per_device_line(
    tokens, out_grad, expert_ids, gate_values, gate_weight, up_weight, down_weight
):
    tok_count, width = tokens.shape
    expert_count = lax.axis_size("expert") * gate_weight.shape[0]
    shard_rows, half = gate_weight.shape[1:]
    dp_count = lax.axis_size("dp")
    expert = lax.axis_index("expert")
    place = jnp.stack([lax.axis_index("dp"), expert]).astype(jnp.int32)
    pair_shard = jnp.concatenate([gate_weight[0], up_weight[0]], axis=1)
    pair_parts = gathered("wp", pair_shard)
    lane = jnp.arange(EXT, dtype=jnp.int32)[None, :]
    dense = jnp.where(lane % expert_count == expert_ids[:, :1], gate_values[:, :1], 0.0)
    dense = dense + jnp.where(
        lane % expert_count == expert_ids[:, 1:], gate_values[:, 1:], 0.0
    )
    high = dense.astype(jnp.bfloat16).astype(jnp.float32)
    ext = jnp.where(
        lane < expert_count, high, jnp.where(lane < 2 * expert_count, dense - high, 0.0)
    )
    grads = jnp.concatenate([out_grad, ext.astype(jnp.bfloat16)], axis=1)
    x_x, x_y = moved("x_x", tokens, "expert", FLIP_X), moved("x_y", tokens, "expert", FLIP_Y)
    g_x, g_y = moved("g_x", grads, "expert", FLIP_X), moved("g_y", grads, "expert", FLIP_Y)
    down_parts = gathered("wd", down_weight[0])
    x_d = moved("x_d", x_x, "expert", FLIP_Y)
    g_d = moved("g_d", g_y, "expert", FLIP_X)
    x_same, g_same = [tokens, x_x, x_y, x_d], [grads, g_x, g_y, g_d]
    tags = ("o", "x", "y", "d")
    x_blocks = x_same + [moved("xs_" + t, v, "seq", SWAP) for t, v in zip(tags, x_same)]
    g_blocks = g_same + [moved("gs_" + t, v, "seq", SWAP) for t, v in zip(tags, g_same)]
    blocks = len(x_blocks)
    rows = blocks * tok_count
    wide = width + EXT
    dma = pltpu.SemaphoreType.DMA

    hidden_out = pl.pallas_call(
        partial(hidden_kernel, blocks=blocks, expert_count=expert_count),
        name="hidden",
        in_specs=[ON_SCALAR] + [ANY] * (2 * blocks + 5),
        out_specs=[ON_CHIP] * 3 + [ANY] * ROLES,
        out_shape=[shape_of((rows, half), jnp.float32)] * 3
        + [shape_of((half, shard_rows))] * ROLES,
        scratch_shapes=[
            pltpu.VMEM((rows, width), jnp.bfloat16),
            pltpu.VMEM((rows, wide), jnp.bfloat16),
            pltpu.VMEM((width, 2 * half), jnp.bfloat16),
            pltpu.VMEM((rows, half), jnp.bfloat16),
            pltpu.VMEM((dp_count, half, shard_rows), jnp.bfloat16),
            dma((4 + 2 * blocks,)),
        ],
    )(place, *x_blocks, *g_blocks, *pair_parts)
    factors, down_roles = hidden_out[:3], hidden_out[3:]
    down_total = scattered("rd", down_roles)

    grads_out = pl.pallas_call(
        partial(grads_kernel, blocks=blocks, expert_count=expert_count),
        name="grads",
        in_specs=[ON_SCALAR] + [ANY] * (2 * blocks + 5) + [ON_CHIP] * 3,
        out_specs=[ON_CHIP] * 2 + [ANY] * ROLES,
        out_shape=[shape_of((rows, 2 * half)), shape_of((rows, EXT))]
        + [shape_of((2 * half, shard_rows))] * ROLES,
        scratch_shapes=[
            pltpu.VMEM((rows, width), jnp.bfloat16),
            pltpu.VMEM((rows, wide), jnp.bfloat16),
            pltpu.VMEM((width, half), jnp.bfloat16),
            pltpu.VMEM((dp_count, 2 * half, shard_rows), jnp.bfloat16),
            dma((4 + 2 * blocks,)),
        ],
    )(place, *x_blocks, *g_blocks, *down_parts, *factors)
    pair, inner, pair_roles = grads_out[0], grads_out[1], grads_out[2:]
    pair_total = scattered("rp", pair_roles)

    same, other = pl.pallas_call(
        back_kernel,
        name="back",
        in_specs=[ON_SCALAR] + [ANY] * 5 + [ON_CHIP] * 2,
        out_specs=[ON_CHIP] * 2,
        out_shape=[shape_of((rows // 2, wide))] * 2,
        scratch_shapes=[pltpu.VMEM((width, 2 * half), jnp.bfloat16), dma((4,))],
    )(place, *pair_parts, pair, inner)
    met = moved("bs", other, "seq", SWAP)
    home = []
    for number, pairs in enumerate((None, FLIP_X, FLIP_Y, FLIP_XY)):
        span = slice(number * tok_count, (number + 1) * tok_count)
        summed = same[span].astype(jnp.float32) + met[span].astype(jnp.float32)
        lane_w = jnp.arange(wide, dtype=jnp.int32)[None, :]
        part = summed.astype(jnp.bfloat16)
        if pairs is not None:
            part = moved("b" + tags[number], part, "expert", pairs)
        home.append(part.astype(jnp.float32))
    in_grad = (home[0] + home[1] + home[2] + home[3])[:, :width].astype(jnp.bfloat16)
    gate_grads = 0.0
    for number, part in enumerate(home):
        value = part[:, width : width + 1] + part[:, width + 1 : width + 2]
        gate_grads = gate_grads + jnp.where(expert_ids == (expert ^ number), value, 0.0)
    return (
        in_grad,
        gate_grads,
        pair_total[:, :half][None],
        pair_total[:, half:][None],
        down_total[None],
    )


def route_slots(block_ids, expert_count, capacity):
    flat_ids = block_ids.reshape(-1)
    onehot = (flat_ids[:, None] == jnp.arange(expert_count, dtype=jnp.int32)[None, :]).astype(
        jnp.int32
    )
    position = jnp.sum((jnp.cumsum(onehot, axis=0) - 1) * onehot, axis=1)
    return flat_ids * capacity + position


def expert_half(routed, grads_in, gate_vals, gate_cols, up_cols, down_cols):
    contract_last = (((1,), (1,)), ((), ()))
    gate_pre = jnp.dot(routed, gate_cols, preferred_element_type=jnp.float32)
    up_pre = jnp.dot(routed, up_cols, preferred_element_type=jnp.float32)
    sigmoid_val = jax.nn.sigmoid(gate_pre)
    activated = gate_pre * sigmoid_val
    hidden = (activated * up_pre).astype(jnp.bfloat16)
    produced = lax.dot_general(hidden, down_cols, contract_last, preferred_element_type=jnp.float32)
    gate_inner = jnp.sum(grads_in.astype(jnp.float32) * produced, axis=1)
    scaled = (gate_vals[:, None] * grads_in.astype(jnp.float32)).astype(jnp.bfloat16)
    hidden_grad = jnp.dot(scaled, down_cols, preferred_element_type=jnp.float32)
    gate_grad = (
        hidden_grad * up_pre * sigmoid_val * (1.0 + gate_pre * (1.0 - sigmoid_val))
    ).astype(jnp.bfloat16)
    up_grad = (hidden_grad * activated).astype(jnp.bfloat16)
    back_sum = lax.dot_general(
        gate_grad, gate_cols, contract_last, preferred_element_type=jnp.float32
    )
    back_sum = back_sum + lax.dot_general(
        up_grad, up_cols, contract_last, preferred_element_type=jnp.float32
    )
    return (hidden, scaled, gate_grad, up_grad, back_sum.astype(jnp.bfloat16), gate_inner)


def per_device(tokens, out_grad, expert_ids, gate_values, gate_weight, up_weight, down_weight):
    tok_count, model_width = tokens.shape
    expert_span = lax.axis_size("expert")
    seq_count = lax.axis_size("seq")
    expert_count = expert_span * gate_weight.shape[0]
    capacity = min(tok_count, 3 * tok_count // expert_span)
    half_width = gate_weight.shape[2]
    slot_index = route_slots(expert_ids, expert_count, capacity)
    pair_ids = jnp.arange(2 * tok_count, dtype=jnp.int32)
    sources = (
        jnp.full((expert_count * capacity,), 2 * tok_count, jnp.int32).at[slot_index].set(pair_ids)
    )
    token_source = sources // 2
    send_rows = jnp.take(tokens, token_source, axis=0, mode="fill", fill_value=0).reshape(
        expert_count, capacity, model_width
    )
    send_grads = jnp.take(out_grad, token_source, axis=0, mode="fill", fill_value=0).reshape(
        expert_count, capacity, model_width
    )
    send_gates = jnp.take(
        gate_values.reshape(-1), sources, axis=0, mode="fill", fill_value=0
    ).reshape(expert_count, capacity)
    full_gate, full_up, full_down = (
        lax.all_gather(gate_weight[0], "dp", axis=0, tiled=True),
        lax.all_gather(up_weight[0], "dp", axis=0, tiled=True),
        lax.all_gather(down_weight[0], "dp", axis=0, tiled=True),
    )

    def duplicate(source_array):
        widened = jnp.broadcast_to(
            source_array[:, None], (source_array.shape[0], seq_count) + source_array.shape[1:]
        )
        return widened.reshape((source_array.shape[0] * seq_count,) + source_array.shape[1:])

    got_rows, got_grads, got_gates = (
        lax.all_to_all(
            duplicate(send_rows), ("expert", "seq"), split_axis=0, concat_axis=0, tiled=True
        ),
        lax.all_to_all(
            duplicate(send_grads), ("expert", "seq"), split_axis=0, concat_axis=0, tiled=True
        ),
        lax.all_to_all(
            duplicate(send_gates).astype(jnp.bfloat16),
            ("expert", "seq"),
            split_axis=0,
            concat_axis=0,
            tiled=True,
        ).astype(jnp.float32),
    )
    routed_all = got_rows.reshape(-1, model_width)
    grads_all = got_grads.reshape(-1, model_width)
    gates_all = got_gates.reshape(-1)
    hidden, scaled, gate_grad, up_grad, back_grad, gate_inner = expert_half(
        routed_all, grads_all, gates_all, full_gate, full_up, full_down
    )
    contract_first = (((0,), (0,)), ((), ()))
    gate_term = lax.dot_general(
        routed_all, gate_grad, contract_first, preferred_element_type=jnp.float32
    )
    up_term = lax.dot_general(
        routed_all, up_grad, contract_first, preferred_element_type=jnp.float32
    )
    down_term = lax.dot_general(scaled, hidden, contract_first, preferred_element_type=jnp.float32)
    summed_grads = lax.psum_scatter(
        jnp.concatenate([gate_term, up_term, down_term], axis=1).astype(jnp.bfloat16),
        "dp",
        scatter_dimension=0,
        tiled=True,
    ).astype(jnp.float32)
    back_parts, inner_parts = (
        lax.all_to_all(
            back_grad.reshape(expert_count * seq_count, capacity, model_width),
            ("expert", "seq"),
            split_axis=0,
            concat_axis=0,
            tiled=True,
        ),
        lax.all_to_all(
            gate_inner.reshape(expert_count * seq_count, capacity).astype(jnp.bfloat16),
            ("expert", "seq"),
            split_axis=0,
            concat_axis=0,
            tiled=True,
        ).astype(jnp.float32),
    )
    back_parts = back_parts.reshape(expert_count, seq_count, capacity, model_width)
    slot_grad = jnp.sum(back_parts.astype(jnp.float32), axis=1).astype(jnp.bfloat16)
    slot_inner = jnp.sum(inner_parts.reshape(expert_count, seq_count, capacity), axis=1)
    picked = slot_grad.reshape(-1, model_width)[slot_index].reshape(tok_count, 2, model_width)
    in_grad = jnp.sum(picked.astype(jnp.float32), axis=1).astype(jnp.bfloat16)
    gate_grads = slot_inner.reshape(-1)[slot_index].reshape(tok_count, 2)
    gate_weight_grad = summed_grads[:, :half_width].astype(jnp.bfloat16)[None]
    up_weight_grad = summed_grads[:, half_width : 2 * half_width].astype(jnp.bfloat16)[None]
    down_weight_grad = summed_grads[:, 2 * half_width :].astype(jnp.bfloat16)[None]
    return (in_grad, gate_grads, gate_weight_grad, up_weight_grad, down_weight_grad)


def on_a_line(mesh):
    return dict(mesh.shape) == {"dp": 4, "expert": 4, "seq": 2}


def solution(mesh):
    return jax.shard_map(
        per_device_line if on_a_line(mesh) else per_device,
        mesh=mesh,
        in_specs=(
            P(("dp", "expert", "seq"), None),
            P(("dp", "expert", "seq"), None),
            P(("dp", "expert", "seq"), None),
            P(("dp", "expert", "seq"), None),
            P("expert", "dp", "seq"),
            P("expert", "dp", "seq"),
            P("expert", "dp", "seq"),
        ),
        out_specs=(
            P(("dp", "expert", "seq"), None),
            P(("dp", "expert", "seq"), None),
            P("expert", "dp", "seq"),
            P("expert", "dp", "seq"),
            P("expert", "dp", "seq"),
        ),
        check_vma=False,
    )
```
